32 devices in a mesh: frame: 8 (over z, x), head: 4 (over y, core).
Axes of the slice: x: 2, y: 2, z: 4, core: 2. Of those that a mesh axis runs over, the one named last changes fastest.
Arguments:
- tokens: bfloat16 [8, 576, 640], P('frame', 'head'), may hold values from -6 to 6
- ln_gain: float32 [2, 640], replicated, may hold values from 0.25 to 1.75
- qkv_weight: bfloat16 [2, 640, 1920], replicated, may hold values from -6 to 6
- out_weight: bfloat16 [2, 640, 640], replicated, may hold values from -0.3125 to 0.3125
Outputs:
- latents: bfloat16 [8, 576, 640], P('frame', 'head')
The draws below stay inside these ranges and needn't reach their ends.
All inputs are finite; a program needn't handle non-finite values.
Results may differ from the reference program's by a relative error of at most 0.033.
The reference program's roundings to bfloat16 on the way (of `x`, `normed`, `qkv`, `probs` and `attended`) count: a program that leaves them out, or rounds other values in their place, can miss the bound.
Values may be sent and summed in bfloat16 or wider, within the bound.
A program may use at most 64 MiB of HBM per device.

```python
import math
import jax
import jax.numpy as jnp
from jax import lax

D = 640
HEADS = 8
HEAD_DIM = 80
TOK = 576
LAYERS = 2
FRAMES = 8


def draw_tokens(key, part):
    key_own = jax.random.fold_in(key, 11)
    own = jax.random.normal(key_own, (FRAMES, TOK, D), jnp.float32)
    values = own
    return jnp.clip(values, -6.0, 6.0).astype(jnp.bfloat16)


def draw_qkv_weight(key, part):
    key_base = jax.random.fold_in(key, 21)
    base = jnp.clip(jax.random.normal(key_base, (LAYERS, D, 3, HEADS, HEAD_DIM), jnp.float32), -4.0, 4.0)
    base = base * (1.5 / math.sqrt(D))
    return jnp.clip(base, -6.0, 6.0).reshape(LAYERS, D, 3 * D).astype(jnp.bfloat16)


def bell_draw(own_key, dims, deviation, most, held_as=jnp.bfloat16):
    entries = deviation * jax.random.normal(own_key, dims, jnp.float32)
    return jnp.clip(entries, min=-most, max=most).astype(held_as)


def setup_inputs(seed: int = 0) -> dict:
    seeds = jax.random.split(jax.random.key(seed), 5)
    return {
        "tokens": draw_tokens(jax.random.fold_in(seeds[4], 71), 0),
        "ln_gain": jnp.clip(1.0 + 0.15 * jax.random.normal(seeds[1], (LAYERS, D), jnp.float32), 0.25, 1.75),
        "qkv_weight": draw_qkv_weight(jax.random.fold_in(seeds[4], 71), 0),
        "out_weight": bell_draw(seeds[3], (LAYERS, D, D), (D // 2) ** -0.5, 0.3125),
    }


def one_layer(x, gain, wqkv, wout):
    frames = x.shape[0]
    xf = x.astype(jnp.float32)
    mean = lax.optimization_barrier(jnp.mean(xf, axis=-1, keepdims=True))
    var = lax.optimization_barrier(jnp.mean((xf - mean) ** 2, axis=-1, keepdims=True))
    normed = ((xf - mean) * lax.rsqrt(var + 1e-05) * gain).astype(jnp.bfloat16)
    qkv = jnp.dot(normed.reshape(frames * TOK, D), wqkv, preferred_element_type=jnp.float32)
    qkv = qkv.astype(jnp.bfloat16).reshape(frames, TOK, 3, HEADS, HEAD_DIM)
    scale = HEAD_DIM ** (-0.5)

    def attend(index):
        prev = jnp.maximum(index - 1, 0)
        query = qkv[index, :, 0].astype(jnp.float32)
        keys = jnp.concatenate([qkv[0, :, 1], qkv[prev, :, 1]], axis=0).astype(jnp.float32)
        values = jnp.concatenate([qkv[0, :, 2], qkv[prev, :, 2]], axis=0).astype(jnp.float32)
        scores = jnp.einsum('thd,shd->hts', query, keys) * scale
        top = lax.optimization_barrier(jnp.max(scores, axis=-1, keepdims=True))
        expo = jnp.exp(scores - top)
        probs = (expo / lax.optimization_barrier(jnp.sum(expo, axis=-1, keepdims=True))).astype(jnp.bfloat16)
        attended = jnp.einsum('hts,shd->thd', probs.astype(jnp.float32), values)
        return attended.astype(jnp.bfloat16).reshape(TOK, D)
    attended = lax.map(attend, jnp.arange(frames, dtype=jnp.int32))
    proj = jnp.dot(attended.reshape(frames * TOK, D), wout, preferred_element_type=jnp.float32)
    return (xf + proj.reshape(frames, TOK, D)).astype(jnp.bfloat16)

def reference(tokens, ln_gain, qkv_weight, out_weight):
    x = tokens
    for layer in range(LAYERS):
        x = one_layer(x, ln_gain[layer], qkv_weight[layer], out_weight[layer])
    return x
```

```python
import functools
import math
import jax
import jax.numpy as jnp
from jax import lax
from jax.experimental import pallas as pl
from jax.experimental.pallas import tpu as pltpu
from jax.sharding import PartitionSpec as P

HEADS = 8
HEAD_DIM = 80
PAD = 128
LAYERS = 2
CHUNKS = 3
SCALE2 = HEAD_DIM ** (-0.5) * math.log2(math.e)
MESH = pl.DeviceIdType.MESH
CHILD, MATE, ACROSS, RELAY, EXTRA = range(5)


def kernel(nf, tok, gain, wqkv_hbm, wout_hbm, out, wraw, wpad, wo, nb, own, xs, q, kv, att,
           wsem, osem, ssem, rsem):
    f = lax.axis_index("frame")
    h = lax.axis_index("head")
    rows, width = own.shape[1:]
    step = rows // CHUNKS
    mate = h + 1 - 2 * (h % 2)
    across = (h + 2) % 4
    diag = (mate + 2) % 4

    barrier = pltpu.get_barrier_semaphore()
    for hh in (mate, across):
        pl.semaphore_signal(barrier, inc=1, device_id=(f, hh), device_id_type=MESH)
    for d in (-2, -1, 1, 2):
        @pl.when((f + d >= 0) & (f + d < nf))
        def _():
            pl.semaphore_signal(barrier, inc=1, device_id=(f + d, h), device_id_type=MESH)

    def weight_copy(l):
        return pltpu.make_async_copy(wqkv_hbm.at[l], wraw.at[l], wsem.at[l])

    def wout_copy(l, j):
        return pltpu.make_async_copy(wout_hbm.at[l, pl.ds(j * HEAD_DIM, HEAD_DIM)],
                                     wo.at[l, pl.ds(j * PAD, HEAD_DIM)], osem.at[l, j])

    for l in range(LAYERS):
        weight_copy(l).start()
        for j in range(HEADS):
            wout_copy(l, j).start()

    def norm(l, xf):
        mean = jnp.mean(xf, axis=-1, keepdims=True)
        cen = xf - mean
        var = jnp.mean(cen * cen, axis=-1, keepdims=True)
        n = (cen * lax.rsqrt(var + 1e-05) * gain[l:l + 1, :]).astype(jnp.bfloat16)
        own[l] = n

        @pl.when(f == 0)
        def _():
            nb[l, 0, h] = n

    def copy(src, l, kind, quarter, c, who, dev):
        return pltpu.make_async_remote_copy(
            src_ref=src, dst_ref=nb.at[l, kind, quarter, pl.ds(c * step, step)],
            send_sem=ssem.at[l, kind, who, c], recv_sem=rsem.at[l, kind, quarter, c],
            device_id=dev, device_id_type=MESH)

    def part(l, kind, quarter, c):
        return nb.at[l, kind, quarter, pl.ds(c * step, step)]

    def landed(l, kind, quarter, c):
        copy(part(l, kind, quarter, c), l, kind, quarter, c, MATE, (f, mate)).wait_recv()

    def spread(l, kind, c):
        src = part(l, kind, h, c)
        copy(src, l, kind, h, c, ACROSS, (f, across)).start()
        copy(src, l, kind, h, c, MATE, (f, mate)).start()

    def first_step(l, c):
        @pl.when(f > 0)
        def _():
            landed(l, 0, h, c)
        src = part(l, 0, h, c)

        @pl.when(f + 2 < nf)
        def _():
            copy(src, l, 0, h, c, CHILD, (f + 2, h)).start()

        @pl.when(f == 0)
        def _():
            copy(src, l, 0, h, c, EXTRA, (f + 1, h)).start()
        spread(l, 0, c)

    def send_prev(l):
        @pl.when((f > 0) & (f + 1 < nf))
        def _():
            for c in range(CHUNKS):
                copy(own.at[l, pl.ds(c * step, step)], l, 1, h, c, CHILD, (f + 1, h)).start()

    def prev_step(l, c):
        landed(l, 1, h, c)
        spread(l, 1, c)

    def relay(l, kind):
        for c in range(CHUNKS):
            landed(l, kind, across, c)
            copy(part(l, kind, across, c), l, kind, across, c, RELAY, (f, mate)).start()

    def mate_landed(l, kind):
        for quarter in (mate, diag):
            for c in range(CHUNKS):
                landed(l, kind, quarter, c)

    def drain(l):
        def one(kind, who, dev):
            for c in range(CHUNKS):
                copy(part(l, kind, h, c), l, kind, h, c, who, dev).wait_send()

        def group(kind):
            one(kind, MATE, (f, mate))
            one(kind, ACROSS, (f, across))
            one(kind, RELAY, (f, mate))
        group(0)

        @pl.when(f >= 2)
        def _():
            group(1)

        @pl.when(f + 2 < nf)
        def _():
            one(0, CHILD, (f + 2, h))

        @pl.when(f == 0)
        def _():
            one(0, EXTRA, (f + 1, h))

        @pl.when((f > 0) & (f + 1 < nf))
        def _():
            one(1, CHILD, (f + 1, h))

    def widen(l):
        weight_copy(l).wait()

        @pl.loop(0, width // 64)
        def _(i):
            r = pl.ds(pl.multiple_of(i * 64, 64), 64)
            w = wraw[l, r, :]
            zero = jnp.zeros((64, PAD - HEAD_DIM), jnp.bfloat16)
            for j in range(3 * HEADS):
                wpad[l, r, j * PAD:j * PAD + PAD] = jnp.concatenate(
                    [w[:, j * HEAD_DIM:(j + 1) * HEAD_DIM], zero], axis=1)
        for j in range(HEADS):
            wo[l, j * PAD + HEAD_DIM:(j + 1) * PAD, :] = jnp.zeros((PAD - HEAD_DIM, width), jnp.bfloat16)
            wout_copy(l, j).wait()

    def query(l):
        @pl.loop(0, HEADS * PAD // 256)
        def _(i):
            cols = pl.ds(pl.multiple_of(i * 256, 256), 256)
            q[:, cols] = jnp.dot(own[l], wpad[l, :, cols],
                                 preferred_element_type=jnp.float32).astype(jnp.bfloat16)

    def keys_values(l, kind):
        count = 4 * rows

        @pl.loop(0, 2 * HEADS * PAD // 256)
        def _(i):
            cols = pl.ds(pl.multiple_of(i * 256, 256), 256)
            wcols = pl.ds(pl.multiple_of(HEADS * PAD + i * 256, 256), 256)
            n = nb[l, kind].reshape(count, width)
            kv[kind * count:(kind + 1) * count, cols] = jnp.dot(
                n, wpad[l, :, wcols], preferred_element_type=jnp.float32).astype(jnp.bfloat16)

    def attend(count, hook):
        @pl.loop(0, HEADS // 2)
        def _(i):
            if hook is not None:
                @pl.when(i == HEADS // 2 - 1)
                def _():
                    hook()
            for j in range(2):
                cols = pl.ds(pl.multiple_of(i * (2 * PAD) + j * PAD, PAD), PAD)
                vcols = pl.ds(pl.multiple_of(HEADS * PAD + i * (2 * PAD) + j * PAD, PAD), PAD)
                s = lax.dot_general(q[:, cols], kv[:count, cols], (((1,), (1,)), ((), ())),
                                    preferred_element_type=jnp.float32)
                top = jnp.max(s, axis=-1, keepdims=True)
                e = jnp.exp2((s - top) * SCALE2)
                p = (e * (1.0 / jnp.sum(e, axis=-1, keepdims=True))).astype(jnp.bfloat16)
                att[:, cols] = jnp.dot(p, kv[:count, vcols],
                                       preferred_element_type=jnp.float32).astype(jnp.bfloat16)

    def first_steps(l):
        for c in range(CHUNKS):
            first_step(l, c)

    xf = tok[0].astype(jnp.float32)
    norm(0, xf)
    xs[...] = xf
    near = 2 + ((f > 0).astype(jnp.int32) + (f > 1).astype(jnp.int32)
                + (f < nf - 1).astype(jnp.int32) + (f < nf - 2).astype(jnp.int32))
    pl.semaphore_wait(barrier, near)

    for l in range(LAYERS):
        send_prev(l)
        if l == 0:
            @pl.when(f == 0)
            def _():
                first_steps(0)
            widen(0)
            query(0)

            @pl.when((f == 1))
            def _():
                first_steps(0)

            @pl.when((f == 2) | (f == 3))
            def _():
                for c in range(CHUNKS):
                    first_step(0, c)
                    prev_step(0, c)

            @pl.when(f >= 4)
            def _():
                for c in range(CHUNKS):
                    prev_step(0, c)
                first_steps(0)

            @pl.when(f >= 2)
            def _():
                relay(0, 1)
            relay(0, 0)

            @pl.when(f >= 2)
            def _():
                mate_landed(0, 1)
                keys_values(0, 1)
            mate_landed(0, 0)
            keys_values(0, 0)
        else:
            @pl.when(f == 0)
            def _():
                first_steps(l)
            query(l)
            relay(l, 0)
            mate_landed(l, 0)
            keys_values(l, 0)

            @pl.when(f >= 2)
            def _():
                for c in range(CHUNKS):
                    prev_step(l, c)
                relay(l, 1)
                mate_landed(l, 1)
                keys_values(l, 1)

        def ahead():
            @pl.when(f > 0)
            def _():
                first_steps(l + 1)

        hook = ahead if l + 1 < LAYERS else None
        if l == 0:
            widen(1)

        @pl.when(f < 2)
        def _():
            attend(4 * rows, hook)

        @pl.when(f >= 2)
        def _():
            attend(8 * rows, hook)

        proj = jnp.dot(att[...], wo[l], preferred_element_type=jnp.float32)
        x = (xs[...] + proj).astype(jnp.bfloat16)
        if l + 1 < LAYERS:
            xf = x.astype(jnp.float32)
            xs[...] = xf
            norm(l + 1, xf)
        else:
            out[0] = x
    for l in range(LAYERS):
        drain(l)


def shards(nf, tokens, ln_gain, qkv_weight, out_weight):
    _, rows, width = tokens.shape
    bf = jnp.bfloat16
    vmem = pl.BlockSpec(memory_space=pltpu.VMEM)
    hbm = pl.BlockSpec(memory_space=pl.ANY)
    return pl.pallas_call(
        functools.partial(kernel, nf),
        out_shape=jax.ShapeDtypeStruct(tokens.shape, bf),
        in_specs=[vmem, vmem, hbm, hbm],
        out_specs=vmem,
        scratch_shapes=[
            pltpu.VMEM((LAYERS, width, 3 * width), bf),
            pltpu.VMEM((LAYERS, width, 3 * HEADS * PAD), bf),
            pltpu.VMEM((LAYERS, HEADS * PAD, width), bf),
            pltpu.VMEM((LAYERS, 2, 4, rows, width), bf),
            pltpu.VMEM((LAYERS, rows, width), bf),
            pltpu.VMEM((rows, width), jnp.float32),
            pltpu.VMEM((rows, HEADS * PAD), bf),
            pltpu.VMEM((8 * rows, 2 * HEADS * PAD), bf),
            pltpu.VMEM((rows, HEADS * PAD), bf),
            pltpu.SemaphoreType.DMA((LAYERS,)),
            pltpu.SemaphoreType.DMA((LAYERS, HEADS)),
            pltpu.SemaphoreType.DMA((LAYERS, 2, 5, CHUNKS)),
            pltpu.SemaphoreType.DMA((LAYERS, 2, 4, CHUNKS)),
        ],
        compiler_params=pltpu.CompilerParams(
            collective_id=0, has_side_effects=True, vmem_limit_bytes=56 * 1024 * 1024),
    )(tokens, ln_gain, qkv_weight, out_weight)


def solution(mesh):
    placed = (P("frame", "head", None), P(), P(), P())
    return jax.shard_map(
        functools.partial(shards, mesh.shape["frame"]), mesh=mesh, in_specs=placed,
        out_specs=P("frame", "head", None), check_vma=False
    )
```

```python
import functools
import math
import jax
import jax.numpy as jnp
from jax import lax
from jax.experimental import pallas as pl
from jax.experimental.pallas import tpu as pltpu
from jax.sharding import PartitionSpec as P

HEADS = 8
HEAD_DIM = 80
PAD = 128
LAYERS = 2
CHUNKS = 3
GROUP = 4
SCALE2 = HEAD_DIM ** (-0.5) * math.log2(math.e)
MESH = pl.DeviceIdType.MESH
CHILD, MATE, ACROSS, RELAY, EXTRA = range(5)


def kernel(nf, tok, gain, wqkv_hbm, wout_hbm, out, wraw, wpad, wo, nb, own, xs, q, kv, att, acc, top_ref, sum_ref,
           wsem, osem, ssem, rsem):
    f = lax.axis_index("frame")
    h = lax.axis_index("head")
    rows, width = own.shape[1:]
    step = rows // CHUNKS
    mate = h + 1 - 2 * (h % 2)
    across = (h + 2) % 4
    diag = (mate + 2) % 4

    barrier = pltpu.get_barrier_semaphore()
    for hh in (mate, across):
        pl.semaphore_signal(barrier, inc=1, device_id=(f, hh), device_id_type=MESH)
    for d in (-2, -1, 1, 2):
        @pl.when((f + d >= 0) & (f + d < nf))
        def _():
            pl.semaphore_signal(barrier, inc=1, device_id=(f + d, h), device_id_type=MESH)

    def weight_copy(l):
        return pltpu.make_async_copy(wqkv_hbm.at[l], wraw.at[l], wsem.at[l])

    def wout_copy(l, j):
        return pltpu.make_async_copy(wout_hbm.at[l, pl.ds(j * HEAD_DIM, HEAD_DIM)],
                                     wo.at[l, pl.ds(j * PAD, HEAD_DIM)], osem.at[l, j])

    for l in range(LAYERS):
        weight_copy(l).start()
        for j in range(HEADS):
            wout_copy(l, j).start()

    def norm(l, xf):
        mean = jnp.mean(xf, axis=-1, keepdims=True)
        cen = xf - mean
        var = jnp.mean(cen * cen, axis=-1, keepdims=True)
        n = (cen * lax.rsqrt(var + 1e-05) * gain[l:l + 1, :]).astype(jnp.bfloat16)
        own[l] = n

        @pl.when(f == 0)
        def _():
            nb[l, 0, h] = n

    def copy(src, l, kind, quarter, c, who, dev):
        return pltpu.make_async_remote_copy(
            src_ref=src, dst_ref=nb.at[l, kind, quarter, pl.ds(c * step, step)],
            send_sem=ssem.at[l, kind, who, c], recv_sem=rsem.at[l, kind, quarter, c],
            device_id=dev, device_id_type=MESH)

    def part(l, kind, quarter, c):
        return nb.at[l, kind, quarter, pl.ds(c * step, step)]

    def landed(l, kind, quarter, c):
        copy(part(l, kind, quarter, c), l, kind, quarter, c, MATE, (f, mate)).wait_recv()

    def spread(l, kind, c):
        src = part(l, kind, h, c)
        copy(src, l, kind, h, c, ACROSS, (f, across)).start()
        copy(src, l, kind, h, c, MATE, (f, mate)).start()

    def first_step(l, c):
        @pl.when(f > 0)
        def _():
            landed(l, 0, h, c)
        src = part(l, 0, h, c)

        @pl.when(f + 2 < nf)
        def _():
            copy(src, l, 0, h, c, CHILD, (f + 2, h)).start()

        @pl.when(f == 0)
        def _():
            copy(src, l, 0, h, c, EXTRA, (f + 1, h)).start()
        spread(l, 0, c)

    def send_prev(l):
        @pl.when((f > 0) & (f + 1 < nf))
        def _():
            for c in range(CHUNKS):
                copy(own.at[l, pl.ds(c * step, step)], l, 1, h, c, CHILD, (f + 1, h)).start()

    def prev_step(l, c):
        landed(l, 1, h, c)
        spread(l, 1, c)

    def relay(l, kind):
        for c in range(CHUNKS):
            landed(l, kind, across, c)
            copy(part(l, kind, across, c), l, kind, across, c, RELAY, (f, mate)).start()

    def mate_landed(l, kind):
        for quarter in (mate, diag):
            for c in range(CHUNKS):
                landed(l, kind, quarter, c)

    def drain(l):
        def one(kind, who, dev):
            for c in range(CHUNKS):
                copy(part(l, kind, h, c), l, kind, h, c, who, dev).wait_send()

        def group(kind):
            one(kind, MATE, (f, mate))
            one(kind, ACROSS, (f, across))
            one(kind, RELAY, (f, mate))
        group(0)

        @pl.when(f >= 2)
        def _():
            group(1)

        @pl.when(f + 2 < nf)
        def _():
            one(0, CHILD, (f + 2, h))

        @pl.when(f == 0)
        def _():
            one(0, EXTRA, (f + 1, h))

        @pl.when((f > 0) & (f + 1 < nf))
        def _():
            one(1, CHILD, (f + 1, h))

    def widen(l):
        weight_copy(l).wait()

        @pl.loop(0, width // 64)
        def _(i):
            r = pl.ds(pl.multiple_of(i * 64, 64), 64)
            w = wraw[l, r, :]
            zero = jnp.zeros((64, PAD - HEAD_DIM), jnp.bfloat16)
            for j in range(3 * HEADS):
                wpad[l, r, j * PAD:j * PAD + PAD] = jnp.concatenate(
                    [w[:, j * HEAD_DIM:(j + 1) * HEAD_DIM], zero], axis=1)
        for j in range(HEADS):
            wo[l, j * PAD + HEAD_DIM:(j + 1) * PAD, :] = jnp.zeros((PAD - HEAD_DIM, width), jnp.bfloat16)
            wout_copy(l, j).wait()

    def query(l):
        @pl.loop(0, HEADS * PAD // 256)
        def _(i):
            cols = pl.ds(pl.multiple_of(i * 256, 256), 256)
            q[:, cols] = jnp.dot(own[l], wpad[l, :, cols],
                                 preferred_element_type=jnp.float32).astype(jnp.bfloat16)

    half = 4 * rows
    heads_cols = HEADS * PAD

    def keys_values(l, kind, between=None):
        n = nb[l, kind].reshape(half, width)
        for j in range(2):
            if between is not None:
                between[j]()
            kv[kind * half:(kind + 1) * half, j * heads_cols:(j + 1) * heads_cols] = jnp.dot(
                n, wpad[l, :, (j + 1) * heads_cols:(j + 2) * heads_cols],
                preferred_element_type=jnp.float32).astype(jnp.bfloat16)

    def attend(kind, stage, hook=None):
        @pl.loop(0, HEADS // GROUP)
        def _(i):
            if hook is not None:
                @pl.when(i == HEADS // GROUP - 1)
                def _():
                    hook()
            keys = slice(kind * half, (kind + 1) * half)
            for j in range(GROUP):
                cols = pl.ds(pl.multiple_of((i * GROUP + j) * PAD, PAD), PAD)
                vcols = pl.ds(pl.multiple_of(heads_cols + (i * GROUP + j) * PAD, PAD), PAD)
                head = i * GROUP + j
                s = lax.dot_general(q[:, cols], kv[keys, cols], (((1,), (1,)), ((), ())),
                                    preferred_element_type=jnp.float32)
                top = jnp.max(s, axis=-1, keepdims=True)
                if stage == "last":
                    before = top_ref[head]
                    top = jnp.maximum(top, before)
                e = jnp.exp2((s - top) * SCALE2)
                total = jnp.sum(e, axis=-1, keepdims=True)
                part_out = jnp.dot(e.astype(jnp.bfloat16), kv[keys, vcols],
                                   preferred_element_type=jnp.float32)
                if stage == "first":
                    top_ref[head] = top
                    sum_ref[head] = total
                    acc[:, cols] = part_out
                    continue
                if stage == "last":
                    fade = jnp.exp2((before - top) * SCALE2)
                    total = total + sum_ref[head] * fade
                    part_out = part_out + acc[:, cols] * fade
                att[:, cols] = (part_out * (1.0 / total)).astype(jnp.bfloat16)

    def first_steps(l):
        for c in range(CHUNKS):
            first_step(l, c)

    def prev_steps(l):
        for c in range(CHUNKS):
            prev_step(l, c)

    def both_steps(l):
        for c in range(CHUNKS):
            first_step(l, c)
            prev_step(l, c)

    def two_halves_first(l):
        relay(l, 1)
        mate_landed(l, 1)
        keys_values(l, 1)
        attend(1, "first", functools.partial(relay, l, 0))
        mate_landed(l, 0)
        keys_values(l, 0)

        @pl.when(f + 2 < nf)
        def _():
            first_steps(l + 1)
        attend(0, "last")

    def two_halves_second(l):
        relay(l, 0)
        mate_landed(l, 0)
        keys_values(l, 0, [functools.partial(prev_step, l, c) for c in range(2)])
        prev_step(l, 2)
        attend(0, "first", functools.partial(relay, l, 1))
        mate_landed(l, 1)
        keys_values(l, 1)
        attend(1, "last")

    def one_half(l):
        relay(l, 0)
        mate_landed(l, 0)
        keys_values(l, 0)
        attend(0, "only")

    xf = tok[0].astype(jnp.float32)
    norm(0, xf)
    xs[...] = xf
    near = 2 + ((f > 0).astype(jnp.int32) + (f > 1).astype(jnp.int32)
                + (f < nf - 1).astype(jnp.int32) + (f < nf - 2).astype(jnp.int32))
    pl.semaphore_wait(barrier, near)

    for l in range(LAYERS):
        send_prev(l)

        if l == 0:
            @pl.when(f == 0)
            def _():
                first_steps(l)
            widen(0)
        else:
            @pl.when((f < 2) | (f + 2 >= nf))
            def _():
                first_steps(l)
        query(l)
        if l == 0:
            @pl.when((f == 0) | (f >= 4))
            def _():
                widen(1)

        if l == 0:
            @pl.when(f == 1)
            def _():
                first_steps(l)

            @pl.when((f == 2) | (f == 3))
            def _():
                both_steps(l)

            @pl.when(f >= 4)
            def _():
                prev_steps(l)
                first_steps(l)

            @pl.when((f > 0) & (f < 4))
            def _():
                widen(1)

        @pl.when(f < 2)
        def _():
            one_half(l)

        @pl.when(f >= 2)
        def _():
            if l == 0:
                two_halves_first(l)
            else:
                two_halves_second(l)

        proj = jnp.dot(att[...], wo[l], preferred_element_type=jnp.float32)
        x = (xs[...] + proj).astype(jnp.bfloat16)
        if l + 1 < LAYERS:
            xf = x.astype(jnp.float32)
            xs[...] = xf
            norm(l + 1, xf)
        else:
            out[0] = x
    for l in range(LAYERS):
        drain(l)


def shards(nf, tokens, ln_gain, qkv_weight, out_weight):
    _, rows, width = tokens.shape
    bf = jnp.bfloat16
    vmem = pl.BlockSpec(memory_space=pltpu.VMEM)
    hbm = pl.BlockSpec(memory_space=pl.ANY)
    return pl.pallas_call(
        functools.partial(kernel, nf),
        out_shape=jax.ShapeDtypeStruct(tokens.shape, bf),
        in_specs=[vmem, vmem, hbm, hbm],
        out_specs=vmem,
        scratch_shapes=[
            pltpu.VMEM((LAYERS, width, 3 * width), bf),
            pltpu.VMEM((LAYERS, width, 3 * HEADS * PAD), bf),
            pltpu.VMEM((LAYERS, HEADS * PAD, width), bf),
            pltpu.VMEM((LAYERS, 2, 4, rows, width), bf),
            pltpu.VMEM((LAYERS, rows, width), bf),
            pltpu.VMEM((rows, width), jnp.float32),
            pltpu.VMEM((rows, HEADS * PAD), bf),
            pltpu.VMEM((8 * rows, 2 * HEADS * PAD), bf),
            pltpu.VMEM((rows, HEADS * PAD), bf),
            pltpu.VMEM((rows, HEADS * PAD), jnp.float32),
            pltpu.VMEM((HEADS, rows, 1), jnp.float32),
            pltpu.VMEM((HEADS, rows, 1), jnp.float32),
            pltpu.SemaphoreType.DMA((LAYERS,)),
            pltpu.SemaphoreType.DMA((LAYERS, HEADS)),
            pltpu.SemaphoreType.DMA((LAYERS, 2, 5, CHUNKS)),
            pltpu.SemaphoreType.DMA((LAYERS, 2, 4, CHUNKS)),
        ],
        compiler_params=pltpu.CompilerParams(
            collective_id=0, has_side_effects=True, vmem_limit_bytes=56 * 1024 * 1024),
    )(tokens, ln_gain, qkv_weight, out_weight)


def solution(mesh):
    placed = (P("frame", "head", None), P(), P(), P())
    return jax.shard_map(
        functools.partial(shards, mesh.shape["frame"]), mesh=mesh, in_specs=placed,
        out_specs=P("frame", "head", None), check_vma=False
    )
```

```python
import functools
import math
import jax
import jax.numpy as jnp
from jax import lax
from jax.experimental import pallas as pl
from jax.experimental.pallas import tpu as pltpu
from jax.sharding import PartitionSpec as P

HEADS = 8
HEAD_DIM = 80
PAD = 128
LAYERS = 2
CHUNKS = 3
GROUP = 4
SCALE2 = HEAD_DIM ** (-0.5) * math.log2(math.e)
MESH = pl.DeviceIdType.MESH
CHILD, MATE, ACROSS, RELAY, EXTRA = range(5)


def kernel(nf, tok, gain, wqkv_hbm, wout_hbm, out, wraw, wpad, wo, nb, own, xs, q, kv, att, acc, top_ref, sum_ref,
           wsem, osem, ssem, rsem):
    f = lax.axis_index("frame")
    h = lax.axis_index("head")
    rows, width = own.shape[1:]
    step = rows // CHUNKS
    mate = h + 1 - 2 * (h % 2)
    across = (h + 2) % 4
    diag = (mate + 2) % 4

    barrier = pltpu.get_barrier_semaphore()
    for hh in (mate, across):
        pl.semaphore_signal(barrier, inc=1, device_id=(f, hh), device_id_type=MESH)
    for d in (-2, -1, 1, 2):
        @pl.when((f + d >= 0) & (f + d < nf))
        def _():
            pl.semaphore_signal(barrier, inc=1, device_id=(f + d, h), device_id_type=MESH)

    def weight_copy(l):
        return pltpu.make_async_copy(wqkv_hbm.at[l], wraw.at[l], wsem.at[l])

    def wout_copy(l, j):
        return pltpu.make_async_copy(wout_hbm.at[l, pl.ds(j * HEAD_DIM, HEAD_DIM)],
                                     wo.at[l, pl.ds(j * PAD, HEAD_DIM)], osem.at[l, j])

    for l in range(LAYERS):
        weight_copy(l).start()
        for j in range(HEADS):
            wout_copy(l, j).start()

    def norm(l, xf):
        mean = jnp.mean(xf, axis=-1, keepdims=True)
        cen = xf - mean
        var = jnp.mean(cen * cen, axis=-1, keepdims=True)
        n = (cen * lax.rsqrt(var + 1e-05) * gain[l:l + 1, :]).astype(jnp.bfloat16)
        own[l] = n

        @pl.when(f == 0)
        def _():
            nb[l, 0, h] = n

    def copy(src, l, kind, quarter, c, who, dev):
        return pltpu.make_async_remote_copy(
            src_ref=src, dst_ref=nb.at[l, kind, quarter, pl.ds(c * step, step)],
            send_sem=ssem.at[l, kind, who, c], recv_sem=rsem.at[l, kind, quarter, c],
            device_id=dev, device_id_type=MESH)

    def part(l, kind, quarter, c):
        return nb.at[l, kind, quarter, pl.ds(c * step, step)]

    def landed(l, kind, quarter, c):
        copy(part(l, kind, quarter, c), l, kind, quarter, c, MATE, (f, mate)).wait_recv()

    def spread(l, kind, c):
        src = part(l, kind, h, c)
        copy(src, l, kind, h, c, ACROSS, (f, across)).start()
        copy(src, l, kind, h, c, MATE, (f, mate)).start()

    def first_step(l, c):
        @pl.when(f > 0)
        def _():
            landed(l, 0, h, c)
        src = part(l, 0, h, c)

        @pl.when(f + 2 < nf)
        def _():
            copy(src, l, 0, h, c, CHILD, (f + 2, h)).start()

        @pl.when(f == 0)
        def _():
            copy(src, l, 0, h, c, EXTRA, (f + 1, h)).start()
        spread(l, 0, c)

    def send_prev(l):
        @pl.when((f > 0) & (f + 1 < nf))
        def _():
            for c in range(CHUNKS):
                copy(own.at[l, pl.ds(c * step, step)], l, 1, h, c, CHILD, (f + 1, h)).start()

    def prev_step(l, c):
        landed(l, 1, h, c)
        spread(l, 1, c)

    def relay(l, kind):
        for c in range(CHUNKS):
            landed(l, kind, across, c)
            copy(part(l, kind, across, c), l, kind, across, c, RELAY, (f, mate)).start()

    def mate_landed(l, kind):
        for quarter in (mate, diag):
            for c in range(CHUNKS):
                landed(l, kind, quarter, c)

    def drain(l):
        def one(kind, who, dev):
            for c in range(CHUNKS):
                copy(part(l, kind, h, c), l, kind, h, c, who, dev).wait_send()

        def group(kind):
            one(kind, MATE, (f, mate))
            one(kind, ACROSS, (f, across))
            one(kind, RELAY, (f, mate))
        group(0)

        @pl.when(f >= 2)
        def _():
            group(1)

        @pl.when(f + 2 < nf)
        def _():
            one(0, CHILD, (f + 2, h))

        @pl.when(f == 0)
        def _():
            one(0, EXTRA, (f + 1, h))

        @pl.when((f > 0) & (f + 1 < nf))
        def _():
            one(1, CHILD, (f + 1, h))

    def widen(l):
        weight_copy(l).wait()

        @pl.loop(0, width // 64)
        def _(i):
            r = pl.ds(pl.multiple_of(i * 64, 64), 64)
            w = wraw[l, r, :]
            zero = jnp.zeros((64, PAD - HEAD_DIM), jnp.bfloat16)
            for j in range(3 * HEADS):
                wpad[l, r, j * PAD:j * PAD + PAD] = jnp.concatenate(
                    [w[:, j * HEAD_DIM:(j + 1) * HEAD_DIM], zero], axis=1)
        for j in range(HEADS):
            wo[l, j * PAD + HEAD_DIM:(j + 1) * PAD, :] = jnp.zeros((PAD - HEAD_DIM, width), jnp.bfloat16)
            wout_copy(l, j).wait()

    def query(l):
        @pl.loop(0, HEADS * PAD // 256)
        def _(i):
            cols = pl.ds(pl.multiple_of(i * 256, 256), 256)
            q[:, cols] = jnp.dot(own[l], wpad[l, :, cols],
                                 preferred_element_type=jnp.float32).astype(jnp.bfloat16)

    half = 4 * rows
    heads_cols = HEADS * PAD

    def keys_values(l, kind, between=None):
        n = nb[l, kind].reshape(half, width)
        for j in range(2):
            if between is not None:
                between[j]()
            kv[kind * half:(kind + 1) * half, j * heads_cols:(j + 1) * heads_cols] = jnp.dot(
                n, wpad[l, :, (j + 1) * heads_cols:(j + 2) * heads_cols],
                preferred_element_type=jnp.float32).astype(jnp.bfloat16)

    def attend(kind, stage, hook=None):
        @pl.loop(0, HEADS // GROUP)
        def _(i):
            if hook is not None:
                @pl.when(i == HEADS // GROUP - 1)
                def _():
                    hook()
            keys = slice(kind * half, (kind + 1) * half)
            for j in range(GROUP):
                cols = pl.ds(pl.multiple_of((i * GROUP + j) * PAD, PAD), PAD)
                vcols = pl.ds(pl.multiple_of(heads_cols + (i * GROUP + j) * PAD, PAD), PAD)
                head = i * GROUP + j
                s = lax.dot_general(q[:, cols], kv[keys, cols], (((1,), (1,)), ((), ())),
                                    preferred_element_type=jnp.float32)
                top = jnp.max(s, axis=-1, keepdims=True)
                if stage == "last":
                    before = top_ref[head]
                    top = jnp.maximum(top, before)
                e = jnp.exp2((s - top) * SCALE2)
                total = jnp.sum(e, axis=-1, keepdims=True)
                part_out = jnp.dot(e.astype(jnp.bfloat16), kv[keys, vcols],
                                   preferred_element_type=jnp.float32)
                if stage == "first":
                    top_ref[head] = top
                    sum_ref[head] = total
                    acc[:, cols] = part_out
                    continue
                if stage == "last":
                    fade = jnp.exp2((before - top) * SCALE2)
                    total = total + sum_ref[head] * fade
                    part_out = part_out + acc[:, cols] * fade
                att[:, cols] = (part_out * (1.0 / total)).astype(jnp.bfloat16)

    def first_steps(l):
        for c in range(CHUNKS):
            first_step(l, c)

    def prev_steps(l):
        for c in range(CHUNKS):
            prev_step(l, c)

    def both_steps(l):
        for c in range(CHUNKS):
            first_step(l, c)
            prev_step(l, c)

    def leaf_step(l, c):
        @pl.when((f >= 4) & (f + 2 >= nf))
        def _():
            first_step(l, c)

    def two_halves_first(l):
        relay(l, 1)
        mate_landed(l, 1)
        keys_values(l, 1, [functools.partial(leaf_step, l, c) for c in range(2)])
        leaf_step(l, 2)
        attend(1, "first", functools.partial(relay, l, 0))
        mate_landed(l, 0)
        keys_values(l, 0)

        @pl.when(f + 2 < nf)
        def _():
            first_steps(l + 1)
        attend(0, "last")

    def two_halves_second(l):
        relay(l, 0)
        mate_landed(l, 0)
        keys_values(l, 0, [functools.partial(prev_step, l, c) for c in range(2)])
        prev_step(l, 2)
        attend(0, "first", functools.partial(relay, l, 1))
        mate_landed(l, 1)
        keys_values(l, 1)
        attend(1, "last")

    def one_half(l):
        relay(l, 0)
        mate_landed(l, 0)
        keys_values(l, 0)
        attend(0, "only")

    xf = tok[0].astype(jnp.float32)
    norm(0, xf)
    xs[...] = xf
    near = 2 + ((f > 0).astype(jnp.int32) + (f > 1).astype(jnp.int32)
                + (f < nf - 1).astype(jnp.int32) + (f < nf - 2).astype(jnp.int32))
    pl.semaphore_wait(barrier, near)

    for l in range(LAYERS):
        send_prev(l)

        if l == 0:
            @pl.when(f == 0)
            def _():
                first_steps(l)
            widen(0)
        else:
            @pl.when((f < 2) | (f + 2 >= nf))
            def _():
                first_steps(l)
        query(l)
        if l == 0:
            @pl.when((f == 0) | (f >= 4))
            def _():
                widen(1)

        if l == 0:
            @pl.when(f == 1)
            def _():
                first_steps(l)

            @pl.when((f == 2) | (f == 3))
            def _():
                both_steps(l)

            @pl.when(f >= 4)
            def _():
                prev_steps(l)

            @pl.when((f >= 4) & (f + 2 < nf))
            def _():
                first_steps(l)

            @pl.when((f > 0) & (f < 4))
            def _():
                widen(1)

        @pl.when(f < 2)
        def _():
            one_half(l)

        @pl.when(f >= 2)
        def _():
            if l == 0:
                two_halves_first(l)
            else:
                two_halves_second(l)

        proj = jnp.dot(att[...], wo[l], preferred_element_type=jnp.float32)
        x = (xs[...] + proj).astype(jnp.bfloat16)
        if l + 1 < LAYERS:
            xf = x.astype(jnp.float32)
            xs[...] = xf
            norm(l + 1, xf)
        else:
            out[0] = x
    for l in range(LAYERS):
        drain(l)


def shards(nf, tokens, ln_gain, qkv_weight, out_weight):
    _, rows, width = tokens.shape
    bf = jnp.bfloat16
    vmem = pl.BlockSpec(memory_space=pltpu.VMEM)
    hbm = pl.BlockSpec(memory_space=pl.ANY)
    return pl.pallas_call(
        functools.partial(kernel, nf),
        out_shape=jax.ShapeDtypeStruct(tokens.shape, bf),
        in_specs=[vmem, vmem, hbm, hbm],
        out_specs=vmem,
        scratch_shapes=[
            pltpu.VMEM((LAYERS, width, 3 * width), bf),
            pltpu.VMEM((LAYERS, width, 3 * HEADS * PAD), bf),
            pltpu.VMEM((LAYERS, HEADS * PAD, width), bf),
            pltpu.VMEM((LAYERS, 2, 4, rows, width), bf),
            pltpu.VMEM((LAYERS, rows, width), bf),
            pltpu.VMEM((rows, width), jnp.float32),
            pltpu.VMEM((rows, HEADS * PAD), bf),
            pltpu.VMEM((8 * rows, 2 * HEADS * PAD), bf),
            pltpu.VMEM((rows, HEADS * PAD), bf),
            pltpu.VMEM((rows, HEADS * PAD), jnp.float32),
            pltpu.VMEM((HEADS, rows, 1), jnp.float32),
            pltpu.VMEM((HEADS, rows, 1), jnp.float32),
            pltpu.SemaphoreType.DMA((LAYERS,)),
            pltpu.SemaphoreType.DMA((LAYERS, HEADS)),
            pltpu.SemaphoreType.DMA((LAYERS, 2, 5, CHUNKS)),
            pltpu.SemaphoreType.DMA((LAYERS, 2, 4, CHUNKS)),
        ],
        compiler_params=pltpu.CompilerParams(
            collective_id=0, has_side_effects=True, vmem_limit_bytes=56 * 1024 * 1024),
    )(tokens, ln_gain, qkv_weight, out_weight)


def solution(mesh):
    placed = (P("frame", "head", None), P(), P(), P())
    return jax.shard_map(
        functools.partial(shards, mesh.shape["frame"]), mesh=mesh, in_specs=placed,
        out_specs=P("frame", "head", None), check_vma=False
    )
```
